32 devices in a mesh: comp: 4 (over x, core), mom: 8 (over z, y).
Axes of the slice: x: 2, y: 2, z: 4, core: 2. Of those that a mesh axis runs over, the one named last changes fastest.
Arguments:
- green_guess: float32 [4, 512, 192, 384], P('comp', 'mom'), may hold values from -3 to 3
- green_free: float32 [4, 512, 192, 384], P('comp', 'mom'), may hold values from -3 to 3
- retarded: float32 [512, 192, 384], P('mom'), may hold values from -0.3125 to 0.3125
- momentum_order: int32 [512], replicated, may hold values from 0 to 511, each once
Outputs:
- green_final: float32 [4, 512, 192, 384], P('comp', 'mom')
- self_energy: float32 [4, 512, 192, 384], P('comp', 'mom')
The draws below stay inside these ranges and needn't reach their ends.
Inputs may be any that keep to these rules, and one draw needn't show every extreme that they name: `momentum_order`: a permutation of the lattice momenta 0 to 511.
All inputs are finite; a program needn't handle non-finite values.
Results may differ from the reference program's by a relative error of at most 0.00013.
Values sent between devices are 32-bit elements; how exact they have to be, the bound alone decides.
A program may use at most 192 MiB of HBM per device.

```python
import math
import jax
import jax.numpy as jnp
from jax import lax

COMP = 4
K = 512
L1 = 16
NT = 192
ITERS = 1


def block_levels(rng, extent, cuts, least, top_value):
    def one(position, shards_of):
        steps = jax.random.uniform(jax.random.fold_in(jax.random.fold_in(rng, 6), position), (shards_of,), jnp.float32, least / len(cuts), top_value / len(cuts))
        return jnp.repeat(jnp.exp(steps), extent[position] // shards_of).reshape((-1,) + (1,) * (len(extent) - position - 1))

    level = one(*cuts[0])
    for cut in cuts[1:]:
        level = level * one(*cut)
    return level


def scatter_about(stream_key, shape, spread, bound, shards=(), kind=jnp.bfloat16):
    factor_of = block_levels(stream_key, shape, shards, -0.22, 0.18) if shards else 1.0
    result = jax.random.normal(stream_key, shape, jnp.float32) * spread * factor_of
    return jnp.minimum(jnp.maximum(result, -bound), bound).astype(kind)


def setup_inputs(seed: int = 0) -> dict:
    key_list = jax.random.split(jax.random.key(seed), 5)
    return {
        "green_guess": scatter_about(key_list[0], (COMP, K, NT, 2 * NT), 0.5, 3.0, ((0, 4), (1, 8)), jnp.float32),
        "green_free": scatter_about(key_list[1], (COMP, K, NT, 2 * NT), 0.5, 3.0, ((0, 4), (1, 8)), jnp.float32),
        "retarded": scatter_about(key_list[2], (K, NT, 2 * NT), (2 * NT) ** -0.5, 0.3125, ((0, 8),), jnp.float32),
        "momentum_order": jax.random.permutation(key_list[3], K).astype(jnp.int32),
    }


highest = lax.Precision.HIGHEST

def phase_tables(momentum_order, count, first_len):
    second_len = count // first_len
    site_ids = jnp.arange(count, dtype=jnp.int32)
    site_one = site_ids // second_len
    site_two = site_ids % second_len
    mom_one = momentum_order.astype(jnp.int32) // second_len
    mom_two = momentum_order.astype(jnp.int32) % second_len
    phases = (site_one[:, None] * mom_one[None, :] * second_len + site_two[:, None] * mom_two[None, :] * first_len) % count
    angles = phases.astype(jnp.float32) * (2.0 * math.pi / count)
    norm_factor = 1.0 / math.sqrt(count)
    return (jnp.cos(angles) * norm_factor, jnp.sin(angles) * norm_factor)

def forward_transform(values, cosine, sine_table, half_width):
    full_shape = values.shape
    flattened = values.reshape(full_shape[0], -1)
    with_cos = jnp.dot(cosine, flattened, precision=highest, preferred_element_type=jnp.float32).reshape(full_shape)
    with_sin = jnp.dot(sine_table, flattened, precision=highest, preferred_element_type=jnp.float32).reshape(full_shape)
    real_part = with_cos[..., :half_width] - with_sin[..., half_width:]
    imag_part = with_cos[..., half_width:] + with_sin[..., :half_width]
    return jnp.concatenate([real_part, imag_part], axis=-1)

def inverse_transform(values, cos_back, sin_back, half_width):
    full_shape = values.shape
    flattened = values.reshape(full_shape[0], -1)
    with_cos = jnp.dot(cos_back, flattened, precision=highest, preferred_element_type=jnp.float32).reshape(full_shape)
    with_sin = jnp.dot(sin_back, flattened, precision=highest, preferred_element_type=jnp.float32).reshape(full_shape)
    real_part = with_cos[..., :half_width] + with_sin[..., half_width:]
    imag_part = with_cos[..., half_width:] - with_sin[..., :half_width]
    return jnp.concatenate([real_part, imag_part], axis=-1)

def triple(own_part, second, conj_factor, half_width):
    prod_real = own_part[..., :half_width] * second[..., :half_width] - own_part[..., half_width:] * second[..., half_width:]
    prod_imag = own_part[..., :half_width] * second[..., half_width:] + own_part[..., half_width:] * second[..., :half_width]
    conj_real = conj_factor[..., :half_width]
    conj_imag = conj_factor[..., half_width:]
    real_part = prod_real * conj_real + prod_imag * conj_imag
    imag_part = prod_imag * conj_real - prod_real * conj_imag
    return -jnp.concatenate([real_part, imag_part], axis=-1)

def dyson(sigma_mom, retarded, free_part, half_width):
    ret_real = retarded[..., :half_width]
    ret_imag = retarded[..., half_width:]
    swapped = jnp.concatenate([-sigma_mom[..., half_width:], sigma_mom[..., :half_width]], axis=-1)
    left_prod = jnp.einsum('kij,kjx->kix', ret_real, sigma_mom, precision=highest, preferred_element_type=jnp.float32)
    left_prod = left_prod + jnp.einsum('kij,kjx->kix', ret_imag, swapped, precision=highest, preferred_element_type=jnp.float32)
    turned = jnp.concatenate([left_prod[..., half_width:], -left_prod[..., :half_width]], axis=-1)
    real_part = jnp.einsum('kim,kjm->kij', left_prod, retarded, precision=highest, preferred_element_type=jnp.float32)
    imag_part = jnp.einsum('kim,kjm->kij', turned, retarded, precision=highest, preferred_element_type=jnp.float32)
    return free_part + jnp.concatenate([real_part, imag_part], axis=-1)

def reference(green_guess, green_free, retarded, momentum_order):
    half_width = NT
    row_block = 8
    cosine, sine_table = phase_tables(momentum_order, K, L1)
    cos_back = cosine.T
    sin_back = sine_table.T
    free_by_mom = jnp.moveaxis(green_free, 1, 0)
    current = green_guess
    sigma_out = green_guess

    def one_block(row_piece):
        by_moment = jnp.moveaxis(row_piece, 1, 0)
        in_sites = forward_transform(by_moment, cosine, sine_table, half_width)
        second = jnp.concatenate([in_sites[:, 2:], in_sites[:, :2]], axis=1)
        conj_factor = jnp.flip(in_sites, axis=1)
        sigma_sites = triple(in_sites, second, conj_factor, half_width)
        return inverse_transform(sigma_sites, cos_back, sin_back, half_width)

    def one_moment(inputs_k):
        sigma_k, ret_k, free_k = inputs_k
        ret_many = jnp.broadcast_to(ret_k[None], (COMP, NT, 2 * NT))
        return dyson(sigma_k, ret_many, free_k, half_width)
    for iteration in range(ITERS):
        blocks = current.reshape(COMP, K, NT // row_block, row_block, 2 * NT)
        blocks = jnp.moveaxis(blocks, 2, 0)
        sigma_blocks = lax.map(one_block, blocks)
        sigma_mom = jnp.transpose(sigma_blocks, (1, 2, 0, 3, 4)).reshape(K, COMP, NT, 2 * NT)
        updated = lax.map(one_moment, (sigma_mom, retarded, free_by_mom))
        current = jnp.moveaxis(updated, 0, 1)
        sigma_out = jnp.moveaxis(sigma_mom, 0, 1)
    return (current, sigma_out)
```

```python
import math

import jax
import jax.numpy as jnp
from jax import lax
from jax.sharding import PartitionSpec as P

K = 512
L1 = 16


highest = lax.Precision.HIGH


def partner(x, axis, bit):
    return lax.ppermute(x, axis, [(i, i ^ 1 << bit) for i in range(lax.axis_size(axis))])


def phase_tables(momentum_order, count, first_len):
    second_len = count // first_len
    site_ids = jnp.arange(count, dtype=jnp.int32)
    site_one = site_ids // second_len
    site_two = site_ids % second_len
    mom_one = momentum_order // second_len
    mom_two = momentum_order % second_len
    phases = (
        site_one[:, None] * mom_one[None, :] * second_len
        + site_two[:, None] * mom_two[None, :] * first_len
    ) % count
    angles = phases.astype(jnp.float32) * (2.0 * math.pi / count)
    norm_factor = 1.0 / math.sqrt(count)
    return (jnp.cos(angles) * norm_factor, jnp.sin(angles) * norm_factor)


def forward_transform(values, cosine, sine_table, half_width):
    full_shape = values.shape
    flattened = values.reshape(full_shape[0], -1)
    with_cos = jnp.dot(
        cosine, flattened, precision=highest, preferred_element_type=jnp.float32
    ).reshape(full_shape)
    with_sin = jnp.dot(
        sine_table, flattened, precision=highest, preferred_element_type=jnp.float32
    ).reshape(full_shape)
    real_part = with_cos[..., :half_width] - with_sin[..., half_width:]
    imag_part = with_cos[..., half_width:] + with_sin[..., :half_width]
    return jnp.concatenate([real_part, imag_part], axis=-1)


def inverse_transform(values, cos_back, sin_back, half_width):
    full_shape = values.shape
    flattened = values.reshape(full_shape[0], -1)
    with_cos = jnp.dot(
        cos_back, flattened, precision=highest, preferred_element_type=jnp.float32
    ).reshape(full_shape)
    with_sin = jnp.dot(
        sin_back, flattened, precision=highest, preferred_element_type=jnp.float32
    ).reshape(full_shape)
    real_part = with_cos[..., :half_width] + with_sin[..., half_width:]
    imag_part = with_cos[..., half_width:] - with_sin[..., :half_width]
    return jnp.concatenate([real_part, imag_part], axis=-1)


def triple(own_part, second, conj_factor, half_width):
    prod_real = (
        own_part[..., :half_width] * second[..., :half_width]
        - own_part[..., half_width:] * second[..., half_width:]
    )
    prod_imag = (
        own_part[..., :half_width] * second[..., half_width:]
        + own_part[..., half_width:] * second[..., :half_width]
    )
    conj_real = conj_factor[..., :half_width]
    conj_imag = conj_factor[..., half_width:]
    real_part = prod_real * conj_real + prod_imag * conj_imag
    imag_part = prod_imag * conj_real - prod_real * conj_imag
    return -jnp.concatenate([real_part, imag_part], axis=-1)


def dyson(sigma_mom, retarded, free_part, half_width):
    ret_real = retarded[..., :half_width]
    ret_imag = retarded[..., half_width:]
    swapped = jnp.concatenate([-sigma_mom[..., half_width:], sigma_mom[..., :half_width]], axis=-1)
    left_prod = jnp.einsum(
        "kij,kjx->kix", ret_real, sigma_mom, precision=highest, preferred_element_type=jnp.float32
    )
    left_prod = left_prod + jnp.einsum(
        "kij,kjx->kix", ret_imag, swapped, precision=highest, preferred_element_type=jnp.float32
    )
    turned = jnp.concatenate([left_prod[..., half_width:], -left_prod[..., :half_width]], axis=-1)
    real_part = jnp.einsum(
        "kim,kjm->kij", left_prod, retarded, precision=highest, preferred_element_type=jnp.float32
    )
    imag_part = jnp.einsum(
        "kim,kjm->kij", turned, retarded, precision=highest, preferred_element_type=jnp.float32
    )
    return free_part + jnp.concatenate([real_part, imag_part], axis=-1)


CHUNKS = 3
GROUPS = 4


def exchange(send, axis):
    size = lax.axis_size(axis)
    return [send[0]] + [
        lax.ppermute(send[s], axis, [(i, i ^ s) for i in range(size)]) for s in range(1, size)
    ]


def on_device(green_guess, green_free, retarded, momentum_order):
    mom_count = lax.axis_size("mom")
    me = lax.axis_index("mom")
    width = green_guess.shape[-1]
    half_width = width // 2
    k_local = green_guess.shape[1]
    tile_rows = half_width // mom_count
    rows = tile_rows // CHUNKS
    group = k_local // GROUPS
    cosine, sine_table = phase_tables(momentum_order, K, L1)
    cos_back = cosine.T
    sin_back = sine_table.T
    free_local = green_free[0]
    current = green_guess[0]

    tiled = current.reshape(k_local, mom_count, CHUNKS, rows, width)
    arrived = [
        lax.all_to_all(tiled[:, :, c], "mom", split_axis=1, concat_axis=0, tiled=True)
        for c in range(CHUNKS)
    ]
    pieces = []
    for c in range(CHUNKS):
        in_sites = forward_transform(arrived[c][:, 0], cosine, sine_table, half_width)
        spin_other = partner(in_sites, "comp", 1)
        cross_other = partner(spin_other, "comp", 0)
        sigma_sites = triple(in_sites, spin_other, cross_other, half_width)
        tile = inverse_transform(sigma_sites, cos_back, sin_back, half_width)
        pieces.append(lax.all_to_all(tile.reshape(mom_count, k_local, 1, rows, width), "mom", split_axis=0, concat_axis=2, tiled=True))
    sigma = jnp.stack(pieces, axis=3).reshape(k_local, half_width, width)
    return (dyson(sigma, retarded, free_local, half_width)[None], sigma[None])


def solution(mesh):
    return jax.shard_map(
        on_device,
        mesh=mesh,
        in_specs=(
            P("comp", "mom", None, None),
            P("comp", "mom", None, None),
            P("mom", None, None),
            P(),
        ),
        out_specs=(P("comp", "mom", None, None), P("comp", "mom", None, None)),
        check_vma=False,
    )
```
